256 devices in a mesh: subj: 16 (over z, x_lo), space: 16 (over x_hi, y, core).
Axes of the slice: x: 4 (x_hi: 2, x_lo: 2; x = x_hi * 2 + x_lo), y: 4, z: 8, core: 2. Of those that a mesh axis runs over, the one named last changes fastest.
Arguments:
- template_warped: bfloat16 [32, 256, 256, 256], P('subj', 'space'), may hold values from -6 to 6
- subject_images: bfloat16 [32, 256, 256, 256], P('subj', 'space'), may hold values from -5 to 5.5, as said below
- jacobians: bfloat16 [32, 256, 256, 256], P('subj', 'space'), may hold values from 0.29882812 to 3
- velocity: float32 [256, 256, 256], P('space', 'subj'), may hold values from -6 to 6
Outputs:
- velocity_new: float32 [256, 256, 256], P('space', 'subj')
The draws below stay inside these ranges and needn't reach their ends.
Inputs may be any that keep to these rules, and one draw needn't show every extreme that they name: `subject_images`: intensities of the subjects' scans.
All inputs are finite; a program needn't handle non-finite values.
Results may differ from the reference program's by a relative error of at most 0.0003.
Values sent between devices are 32-bit elements; how exact they have to be, the bound alone decides.
A program may use at most 128 MiB of HBM per device.

```python
import math
import jax
import jax.numpy as jnp
from jax import lax

GRID = 256
SUBJECTS = 32


def draw_subject_images(key, part):
    noise = jax.random.normal(key, (SUBJECTS, GRID, GRID, GRID), jnp.float32)
    noise = jnp.clip(noise, -5.0, 5.0)
    values = noise
    return values.astype(jnp.bfloat16)


def level_of(rng, extent, cuts, least, largest):
    def one(axis_at, blocks):
        draws = jax.random.uniform(jax.random.fold_in(jax.random.fold_in(rng, 6), axis_at), (blocks,), jnp.float32, least / len(cuts), largest / len(cuts))
        return jnp.repeat(jnp.exp(draws), extent[axis_at] // blocks).reshape((-1,) + (1,) * (len(extent) - axis_at - 1))

    loudness = one(*cuts[0])
    for cut in cuts[1:]:
        loudness = loudness * one(*cut)
    return loudness


def bell_draw(key, extent, scale, most, split=(), held_as=jnp.bfloat16):
    loudness = level_of(key, extent, split, -0.22, 0.18) if split else 1.0
    array = jax.random.normal(key, extent, jnp.float32) * scale * loudness
    return jnp.minimum(jnp.maximum(array, -most), most).astype(held_as)


def setup_inputs(seed: int = 0) -> dict:
    splits = jax.random.split(jax.random.key(seed), 5)
    template_warped = bell_draw(splits[0], (SUBJECTS, GRID, GRID, GRID), 1.0, 6.0, ((0, 16), (1, 16)))
    subject_images = draw_subject_images(jax.random.fold_in(splits[4], 71), 0)
    jacobians = jnp.clip(jnp.exp(math.log(3.0) - 2.306499 * jax.random.uniform(splits[2], (SUBJECTS, GRID, GRID, GRID), jnp.float32) ** level_of(splits[2], (SUBJECTS, GRID, GRID, GRID), ((0, 16), (1, 16)), -0.2, 0.2)), 0.29882812, 3.0).astype(jnp.bfloat16)
    velocity = bell_draw(splits[3], (GRID, GRID, GRID), 1.0, 6.0, ((0, 16), (1, 16)), jnp.float32)
    return {"template_warped": template_warped, "subject_images": subject_images, "jacobians": jacobians, "velocity": velocity}


sigma_sq = 0.05
step_size = 0.25
alpha_reach = 16.0


def smoothing_symbol(first, second, third, length):
    def damping(freq):
        turns = (freq % length).astype(jnp.float32)
        return 2.0 - 2.0 * jnp.cos(turns * (2.0 * math.pi / length))
    total = damping(first) + damping(second) + damping(third)
    return 1.0 / (1.0 + alpha_reach * total) ** 2


def reference(template_warped, subject_images, jacobians, velocity):
    length = template_warped.shape[3]

    def add_subject(total, items):
        warped, image, jac = items
        warped32 = warped.astype(jnp.float32)
        slope = (jnp.roll(warped32, -1, axis=2) - jnp.roll(warped32, 1, axis=2)) * 0.5
        term = jac.astype(jnp.float32) * (image.astype(jnp.float32) - warped32) * slope
        return total + term, None

    start = jnp.zeros((length, length, length), jnp.float32)
    total, _ = lax.scan(add_subject, start, (template_warped, subject_images, jacobians))
    force = total * (2.0 / sigma_sq)
    index = jnp.arange(length, dtype=jnp.int32)
    symbol = smoothing_symbol(index[:, None, None], index[None, :, None], index[None, None, :], length)
    spectrum = jnp.fft.fftn(force)
    smoothed = jnp.real(jnp.fft.ifftn(spectrum * symbol))
    return velocity - step_size * (2.0 * velocity - smoothed)
```

```python
import functools

import jax
import jax.numpy as jnp
import numpy as np
from jax import lax
from jax.experimental import pallas as pl
from jax.experimental.pallas import tpu as pltpu
from jax.sharding import PartitionSpec as P

sigma_sq = 0.05
step_size = 0.25
alpha_reach = 16.0

N = 256
RING = 8
f32 = jnp.float32
bf16 = jnp.bfloat16
MESH = pl.DeviceIdType.MESH


def tables():
    half = N // 2
    index = np.arange(N)
    freq = np.where(index <= half, index, index - half)
    angle = (index[:, None] * freq[None, :] % N) * (2.0 * np.pi / N)
    wave = np.where(index[None, :] <= half, np.cos(angle), np.sin(angle))
    weight = np.where((index == 0) | (index == half), 1.0, 2.0) / N
    basis = wave * np.sqrt(weight)[None, :]
    lam = 2.0 - 2.0 * np.cos(2.0 * np.pi * freq / N)
    s, pp = np.divmod(np.arange(N), 16)
    order = (s // 2) * 32 + (pp // 8) * 16 + (s % 2) * 8 + pp % 8

    def split(a):
        a = jnp.asarray(a, f32)
        hi = a.astype(bf16)
        return hi, (a - hi.astype(f32)).astype(bf16)

    def split_np(a):
        hi = a.astype(np.float32).astype(jnp.bfloat16)
        lo = (a - hi.astype(np.float64)).astype(np.float32).astype(jnp.bfloat16)
        return hi, lo

    stack = []
    for a in (basis.T, basis, basis.T[order]):
        stack.extend(split_np(a))
    return np.stack(stack), lam.astype(np.float32), lam[order].astype(np.float32)


def halves(a):
    hi = a.astype(bf16)
    return hi, (a - hi.astype(f32)).astype(bf16)


def dot3(a, b, dims=((1,), (0,))):
    def one(x, y):
        return lax.dot_general(x, y, (dims, ((), ())), preferred_element_type=f32)

    return one(a[0], b[0]) + (one(a[1], b[0]) + one(a[0], b[1]))


def kernel(
    w_hbm, i_hbm, j_hbm, tab_hbm, lam_smem, lamrow_ref, lamcol_ref, out_ref,
    w_v, i_v, j_v, tab, T, zxr, xzr, xpr, xfr, rt, ys, xr, vs, cr, ws, dr,
    in_sem, tab_sem, zx_s, zx_r, xz_s, xz_r, xp_s, xp_r, xf_s, xf_r,
    b_s, b_r, c_s, c_r, d_s, d_r,
):
    s = lax.axis_index("subj")
    j = lax.axis_index("space")
    z = s // 2
    xlo = s % 2
    partner = s + 1 - 2 * xlo

    def dev(ss, jj):
        return {"subj": ss, "space": jj}

    tab_copy = pltpu.make_async_copy(tab_hbm, tab, tab_sem)
    tab_copy.start()

    def loads(g):
        rows = pl.ds(4 * g, 4)
        return [
            pltpu.make_async_copy(h.at[:, rows], v.at[:, rows], in_sem.at[g, a])
            for a, (h, v) in enumerate(((w_hbm, w_v), (i_hbm, i_v), (j_hbm, j_v)))
        ]

    for g in range(4):
        for c in loads(g):
            c.start()

    barrier = pltpu.get_barrier_semaphore()

    @pl.loop(1, 16)
    def _(i):
        pl.semaphore_signal(barrier, inc=1, device_id=dev((s + i) % 16, j), device_id_type=MESH)
        pl.semaphore_signal(barrier, inc=1, device_id=dev(s, (j + i) % 16), device_id_type=MESH)

    def owner(d, t):
        return (z + 7 - t) % RING if d == 0 else (z + 1 + t) % RING

    def toward(d):
        return (s + 2) % 16 if d == 0 else (s + 14) % 16

    def remote(src, dst, ss, rs, ds, dj):
        return pltpu.make_async_remote_copy(
            src_ref=src, dst_ref=dst, send_sem=ss, recv_sem=rs,
            device_id=dev(ds, dj), device_id_type=MESH,
        )

    def rows(start, size):
        return pl.ds(pl.multiple_of(start, 8), size)

    def t_zx(g, t):
        return T.at[pl.ds(4 * g, 4), rows(32 * owner(g % 2, t), 16), :]

    def t_xz(g, t, side):
        return T.at[pl.ds(4 * g, 4), rows(32 * owner(g % 2, t) + 16 + 8 * side, 8), :]

    def zx_first(g):
        return remote(t_zx(g, 0), zxr.at[0, g], zx_s.at[0, g], zx_r.at[0, g], toward(g % 2), j)

    def zx_next(g, t):
        return remote(zxr.at[t - 1, g], zxr.at[t, g], zx_s.at[t, g], zx_r.at[t, g], toward(g % 2), j)

    def xp(g, t):
        return remote(t_xz(g, t, 1 - xlo), xpr.at[t, g], xp_s.at[t, g], xp_r.at[t, g], partner, j)

    def xz_first(g):
        return remote(xpr.at[0, g], xzr.at[0, g], xz_s.at[0, g], xz_r.at[0, g], toward(g % 2), j)

    def xz_next(g, t):
        return remote(xzr.at[t - 1, g], xzr.at[t, g], xz_s.at[t, g], xz_r.at[t, g], toward(g % 2), j)

    def xf(g):
        return remote(
            zxr.at[6, g, :, rows(8 * (1 - xlo), 8), :], xfr.at[g], xf_s.at[g], xf_r.at[g], partner, j
        )

    for g in range(4):
        for c in loads(g):
            c.wait()
        if g == 0:
            tab_copy.wait()

        @pl.loop(4 * g, 4 * g + 4)
        def _(x):
            total = None
            for sub in range(2):
                w = w_v[sub, x].astype(f32)
                slope = pltpu.roll(w, N - 1, 1) - pltpu.roll(w, 1, 1)
                term = j_v[sub, x].astype(f32) * (i_v[sub, x].astype(f32) - w) * slope
                total = term if total is None else total + term
            T[x] = dot3((tab[0], tab[1]), halves(total), ((1,), (1,)))

        if g == 0:
            pl.semaphore_wait(barrier, 30)
        zx_first(g).start()
        xp(g, 0).start()
        xp(g, 1).start()

    @pl.loop(2, 8)
    def _(t):
        for g in range(4):
            xp(g, t).start()

    def xz_step0():
        for g in range(4):
            xp(g, 0).wait_recv()
            xpr[0, g] += t_xz(g, 0, xlo)[...]
            xz_first(g).start()

    def zx_step(t):
        for g in range(4):
            remote(zxr.at[t - 1, g], zxr.at[t - 1, g], zx_s.at[t - 1, g], zx_r.at[t - 1, g], toward(g % 2), j).wait_recv()
            zxr[t - 1, g] += t_zx(g, t)[...]

    def xz_step(t):
        for g in range(4):
            xp(g, t).wait_recv()
            remote(xzr.at[t - 1, g], xzr.at[t - 1, g], xz_s.at[t - 1, g], xz_r.at[t - 1, g], toward(g % 2), j).wait_recv()
            xzr[t - 1, g] += t_xz(g, t, xlo)[...] + xpr[t, g]

    def zx_full(t):
        for g in range(4):
            remote(zxr.at[t - 1, g], zxr.at[t - 1, g], zx_s.at[t - 1, g], zx_r.at[t - 1, g], toward(g % 2), j).wait_recv()
            zxr[t - 1, g] += t_zx(g, t)[...]
            zx_next(g, t).start()

    def xz_full(t):
        for g in range(4):
            xp(g, t).wait_recv()
            remote(xzr.at[t - 1, g], xzr.at[t - 1, g], xz_s.at[t - 1, g], xz_r.at[t - 1, g], toward(g % 2), j).wait_recv()
            xzr[t - 1, g] += t_xz(g, t, xlo)[...] + xpr[t, g]
            xz_next(g, t).start()

    def put(first, x, value):
        for lh in range(2):
            rt[lh, pl.ds(first + x, 8, stride=16), :] = value[:, 128 * lh:128 * lh + 128]

    zx_full(1)
    xz_step0()

    @pl.loop(2, 7)
    def _(t):
        zx_full(t)
        xz_full(t - 1)

    for g in range(4):
        remote(zxr.at[6, g], zxr.at[6, g], zx_s.at[6, g], zx_r.at[6, g], toward(g % 2), j).wait_recv()
        zxr[6, g] += t_zx(g, 7)[...]
        xf(g).start()
    xz_full(6)
    for g in range(4):
        xf(g).wait_recv()
        mine = zxr[6, g, :, rows(8 * xlo, 8), :] + xfr[g]
        for q in range(4):
            put(0, 4 * g + q, mine[q])
    xz_step(7)
    for g in range(4):
        for q in range(4):
            put(128, 4 * g + q, xzr[6, g, q])

    ys[...] = dot3(halves(jnp.concatenate([rt[0], rt[1]], axis=1)), (tab[2], tab[3])).reshape(16, 16, N)

    def space_copy(src, dst, ss, rs, i):
        to = (j + i) % 16
        return remote(src.at[to], dst.at[j], ss.at[i], rs.at[i], s, to)

    def subj_copy(src, dst, ss, rs, i):
        to = (s + i) % 16
        return remote(src.at[to], dst.at[s], ss.at[i], rs.at[i], to, j)

    def back_copy(src, dst, ss, rs, i):
        to = (j + i) % 16
        return remote(src.at[:, rows(16 * to, 16)], dst.at[:, rows(16 * j, 16)], ss.at[i], rs.at[i], s, to)

    def exchange(make, src, dst, ss, rs, me):
        @pl.loop(1, 16)
        def _(i):
            make(src, dst, ss, rs, i).start()

        if make is back_copy:
            dst[:, rows(16 * me, 16)] = src[:, rows(16 * me, 16)]
        else:
            dst[me] = src[me]

        @pl.loop(1, 16)
        def _(i):
            make(src, dst, ss, rs, i).wait_recv()

    exchange(space_copy, ys, xr, b_s, b_r, j)
    spec = dot3((tab[0], tab[1]), halves(xr[...].reshape(N, N)))
    damp = 1.0 + alpha_reach * (lamrow_ref[...] + lamcol_ref[...] + lam_smem[s * 16 + j])
    spec = spec * ((1.0 / sigma_sq) / (damp * damp))
    back = dot3((tab[2], tab[3]), halves(spec))
    field = dot3(halves(back), (tab[0], tab[1]))
    vs[0] = field[:, :128]
    vs[1] = field[:, 128:]

    exchange(back_copy, vs, cr, c_s, c_r, j)
    lane = lax.broadcasted_iota(jnp.int32, (16, 128), 1)
    parts = []
    for lh in range(2):
        a = [cr[lh, pl.ds(x, 16, stride=16), :] for x in range(16)]
        for b in range(3):
            step = 16 << b
            keep = (lane // step) % 2 == 0
            new = list(a)
            for x in range(16):
                if not x & (1 << b):
                    y = x | (1 << b)
                    new[x] = jnp.where(keep, a[x], pltpu.roll(a[y], step, 1))
                    new[y] = jnp.where(keep, pltpu.roll(a[x], 128 - step, 1), a[y])
            a = new
        parts.append(a)
    for d in range(16):
        for x3 in range(2):
            ws[d, :, 128 * x3:128 * x3 + 128] = parts[d // 8][8 * x3 + d % 8]

    exchange(subj_copy, ws, dr, d_s, d_r, s)
    res = dot3(halves(dr[...].reshape(N, N)), (tab[4], tab[5]), ((0,), (0,)))
    out_ref[...] = res.reshape(16, 16, N)

    @pl.loop(0, 7)
    def _(t):
        for g in range(4):
            remote(zxr.at[t, g], zxr.at[t, g], zx_s.at[t, g], zx_r.at[t, g], toward(g % 2), j).wait_send()
            remote(xzr.at[t, g], xzr.at[t, g], xz_s.at[t, g], xz_r.at[t, g], toward(g % 2), j).wait_send()

    @pl.loop(0, 8)
    def _(t):
        for g in range(4):
            xp(g, t).wait_send()

    for g in range(4):
        xf(g).wait_send()

    @pl.loop(1, 16)
    def _(i):
        space_copy(ys, xr, b_s, b_r, i).wait_send()
        back_copy(vs, cr, c_s, c_r, i).wait_send()
        subj_copy(ws, dr, d_s, d_r, i).wait_send()


def body(template_warped, subject_images, jacobians, velocity):
    stack, lam, lam_order = tables()
    dma = pltpu.SemaphoreType.DMA
    any_spec = pl.BlockSpec(memory_space=pl.ANY)
    vmem = pl.BlockSpec(memory_space=pltpu.VMEM)
    block = pltpu.VMEM((16, 16, N), f32)
    flat = pltpu.VMEM((2, N, 128), f32)
    inp = pltpu.VMEM((2, 16, N, N), bf16)
    smoothed = pl.pallas_call(
        kernel,
        out_shape=jax.ShapeDtypeStruct((16, 16, N), f32),
        in_specs=[any_spec] * 4 + [pl.BlockSpec(memory_space=pltpu.SMEM), vmem, vmem],
        out_specs=vmem,
        scratch_shapes=[
            inp, inp, inp,
            pltpu.VMEM((6, N, N), bf16),
            pltpu.VMEM((16, N, N), f32),
            pltpu.VMEM((7, 4, 4, 16, N), f32),
            pltpu.VMEM((7, 4, 4, 8, N), f32),
            pltpu.VMEM((8, 4, 4, 8, N), f32),
            pltpu.VMEM((4, 4, 8, N), f32),
            flat, block, block, flat, flat, block, block,
            dma((4, 3)), dma,
            dma((7, 4)), dma((7, 4)), dma((7, 4)), dma((7, 4)),
            dma((8, 4)), dma((8, 4)), dma((4,)), dma((4,)),
            dma((16,)), dma((16,)), dma((16,)), dma((16,)), dma((16,)), dma((16,)),
        ],
        compiler_params=pltpu.CompilerParams(
            collective_id=0, has_side_effects=True, vmem_limit_bytes=48 << 20
        ),
        name="force_smooth",
    )(
        template_warped, subject_images, jacobians, jnp.asarray(stack),
        jnp.asarray(lam_order), jnp.asarray(lam)[None, :], jnp.asarray(lam)[:, None],
    )
    return velocity - step_size * (2.0 * velocity - smoothed)


def solution(mesh):
    big = P("subj", "space", None, None)
    out = P("space", "subj", None)
    return jax.shard_map(
        body, mesh=mesh, in_specs=(big, big, big, out), out_specs=out, check_vma=False
    )
```

```python
import jax
import jax.numpy as jnp
import numpy as np
from jax import lax
from jax.experimental import pallas as pl
from jax.experimental.pallas import tpu as pltpu
from jax.sharding import PartitionSpec as P

sigma_sq = 0.05
step_size = 0.25
alpha_reach = 16.0

N = 256
RING = 8
f32 = jnp.float32
bf16 = jnp.bfloat16
MESH = pl.DeviceIdType.MESH


ORDER = (
    ("zx", 0, 0, 0), ("zx", 0, 0, 1), ("zx", 0, 1, 0), ("zx", 0, 1, 1), ("zx", 0, 2, 0), ("zx", 0, 2, 1),
    ("xp", 0, 0, 0), ("xp", 1, 1, 0), ("xp", 0, 1, 0), ("xp", 0, 2, 0), ("zx", 1, 0, 0), ("zx", 1, 0, 1),
    ("zx", 0, 3, 0), ("zx", 1, 1, 1), ("xp", 2, 3, 0), ("xp", 0, 3, 0), ("xz", 0, 0, 0), ("xp", 2, 2, 0),
    ("xp", 4, 2, 0), ("xp", 1, 0, 0), ("xp", 1, 2, 0), ("zx", 0, 3, 1), ("zx", 1, 1, 0), ("xp", 1, 3, 0),
    ("xp", 7, 2, 0), ("xz", 0, 1, 1), ("xp", 2, 0, 0), ("xp", 4, 0, 0), ("zx", 1, 2, 0), ("xp", 4, 3, 0),
    ("zx", 2, 0, 0), ("xp", 7, 0, 0), ("zx", 1, 2, 1), ("xp", 2, 1, 0), ("xz", 0, 2, 0), ("xp", 6, 2, 0),
    ("xz", 0, 3, 1), ("xz", 0, 2, 1), ("zx", 2, 1, 1), ("xp", 6, 1, 0), ("zx", 1, 3, 1), ("xz", 1, 0, 0),
    ("xp", 3, 0, 0), ("xp", 3, 2, 0), ("zx", 1, 3, 0), ("zx", 2, 2, 0), ("xz", 0, 3, 0), ("zx", 2, 2, 1),
    ("xz", 1, 2, 0), ("xz", 1, 3, 1), ("xp", 5, 2, 0), ("zx", 3, 0, 0), ("zx", 2, 1, 0), ("xp", 3, 3, 0),
    ("xz", 0, 0, 1), ("zx", 3, 1, 1), ("xz", 0, 1, 0), ("xp", 4, 1, 0), ("xp", 3, 1, 0), ("xp", 5, 1, 0),
    ("xz", 1, 1, 1), ("zx", 2, 3, 1), ("xp", 6, 3, 0), ("xp", 5, 3, 0), ("xz", 2, 0, 0), ("xz", 1, 2, 1),
    ("xz", 2, 3, 1), ("xz", 2, 2, 0), ("xz", 1, 0, 1), ("xp", 6, 0, 0), ("xz", 1, 3, 0), ("xz", 2, 1, 1),
    ("xp", 5, 0, 0), ("xp", 7, 3, 0), ("zx", 2, 0, 1), ("zx", 2, 3, 0), ("xp", 7, 1, 0), ("xz", 1, 1, 0),
    ("zx", 3, 3, 1), ("zf", 0, 1, 0), ("zx", 3, 2, 0), ("xz", 3, 2, 0), ("xz", 2, 0, 1), ("xz", 3, 0, 0),
    ("xz", 2, 3, 0), ("xz", 2, 2, 1), ("xz", 3, 3, 1), ("xz", 3, 1, 1), ("xz", 2, 1, 0), ("zf", 0, 0, 0),
    ("zf", 0, 3, 0), ("zf", 0, 2, 0), ("xf", 0, 2, 0), ("xf", 0, 3, 0), ("xf", 0, 0, 0), ("xf", 0, 1, 0),
)


def tables():
    half = N // 2
    index = np.arange(N)
    freq = np.where(index <= half, index, index - half)
    angle = (index[:, None] * freq[None, :] % N) * (2.0 * np.pi / N)
    wave = np.where(index[None, :] <= half, np.cos(angle), np.sin(angle))
    weight = np.where((index == 0) | (index == half), 1.0, 2.0) / N
    basis = wave * np.sqrt(weight)[None, :]
    lam = 2.0 - 2.0 * np.cos(2.0 * np.pi * freq / N)

    def packed(s, half, q):
        return (s // 2) * 32 + half * 16 + (s % 2) * 8 + q

    s, jj = np.divmod(np.arange(N), 16)
    filtered = packed(s, jj % 2, jj // 2)
    half, s, q = np.arange(N) // 128, np.arange(N) // 8 % 16, np.arange(N) % 8
    gathered = packed(s, half, q)

    def split(a):
        hi = a.astype(np.float32).astype(jnp.bfloat16)
        lo = (a - hi.astype(np.float64)).astype(np.float32).astype(jnp.bfloat16)
        return hi, lo

    stack = []
    for a in (basis.T, basis, basis.T[gathered]):
        stack.extend(split(a))
    shift = np.roll(np.eye(N), 1, axis=0) - np.roll(np.eye(N), -1, axis=0)
    stack.append(shift.astype(jnp.bfloat16))
    damp = 1.0 + alpha_reach * (lam[:, None] + lam[None, :])
    own = np.broadcast_to(alpha_reach * lam[filtered][:, None], (N, 128))
    return np.stack(stack), np.concatenate([damp, own], axis=1).astype(np.float32)


def halves(a):
    hi = a.astype(bf16)
    return hi, (a - hi.astype(f32)).astype(bf16)


def dot3(a, b, dims=((1,), (0,))):
    def one(x, y):
        return lax.dot_general(x, y, (dims, ((), ())), preferred_element_type=f32)

    return one(a[0], b[0]) + (one(a[1], b[0]) + one(a[0], b[1]))


def kernel(
    w_hbm, i_hbm, j_hbm, tab_hbm, damp_hbm, out_ref,
    w_v, i_v, j_v, tab, damp_v, T, zxr, xzr, xpr, rt0, rt1, xr, vs, cr, ws, dr,
    in_sem, tab_sem, damp_sem, zx_s, zx_r, xz_s, xz_r, xp_s, xp_r,
    b0_s, b1_s, b_r, c_s, c_r, d_s, d_r,
):
    s = lax.axis_index("subj")
    j = lax.axis_index("space")
    z = s // 2
    xlo = s % 2
    partner = s + 1 - 2 * xlo

    def dev(ss, jj):
        return {"subj": ss, "space": jj}

    tab_copy = pltpu.make_async_copy(tab_hbm, tab, tab_sem)
    tab_copy.start()

    def loads(g):
        rows = pl.ds(4 * g, 4)
        return [
            pltpu.make_async_copy(h.at[:, rows], v.at[:, rows], in_sem.at[g, a])
            for a, (h, v) in enumerate(((w_hbm, w_v), (i_hbm, i_v), (j_hbm, j_v)))
        ]

    for g in range(4):
        for c in loads(g):
            c.start()
    damp_copy = pltpu.make_async_copy(damp_hbm, damp_v, damp_sem)
    damp_copy.start()

    barrier = pltpu.get_barrier_semaphore()

    @pl.loop(1, 16)
    def _(i):
        pl.semaphore_signal(barrier, inc=1, device_id=dev((s + i) % 16, j), device_id_type=MESH)
        pl.semaphore_signal(barrier, inc=1, device_id=dev(s, (j + i) % 16), device_id_type=MESH)
        pl.semaphore_signal(barrier, inc=1, device_id=dev(partner, (j + i) % 16), device_id_type=MESH)

    def toward(d):
        return (s + 2) % 16 if d == 0 else (s + 14) % 16

    def remote(src, dst, ss, rs, ds, dj):
        return pltpu.make_async_remote_copy(
            src_ref=src, dst_ref=dst, send_sem=ss, recv_sem=rs,
            device_id=dev(ds, dj), device_id_type=MESH,
        )

    def rows(start, size):
        return pl.ds(pl.multiple_of(start, 8), size)

    def hops(g, d):
        return 4 if d == g % 2 else 3

    def owner(d, dist):
        return (z + dist) % RING if d == 0 else (z + RING - dist) % RING

    def t_zx(g, zo):
        return T.at[pl.ds(4 * g, 4), rows(32 * zo, 16), :]

    def t_xz(g, zo, side):
        return T.at[pl.ds(4 * g, 4), rows(32 * zo + 16 + 8 * side, 8), :]

    def piece(d, dist):
        return {4: 0, 3: 1 + d, 2: 3 + d, 1: 5 + d, 0: 7}[dist]

    def piece_owner(k):
        return (z, owner(0, 4), owner(0, 3), owner(1, 3), owner(0, 2), owner(1, 2), owner(0, 1), owner(1, 1))[(k + 1) % 8]

    def xp(g, k):
        return remote(t_xz(g, piece_owner(k), 1 - xlo), xpr.at[k, g], xp_s.at[k, g], xp_r.at[k, g], partner, j)

    def hop(buf, ss, rs, g, d, r, src=None):
        src = buf.at[d, r - 1, g] if src is None else src
        return remote(src, buf.at[d, r, g], ss.at[d, r, g], rs.at[d, r, g], toward(d), j)

    def arrived(buf, ss, rs, g, d, r):
        hop(buf, ss, rs, g, d, r, buf.at[d, r, g]).wait_recv()

    zx = (zxr, zx_s, zx_r)
    xz = (xzr, xz_s, xz_r)

    def zx_send(g, d, r):
        own = t_zx(g, owner(d, hops(g, d) - r))
        if r == 0:
            hop(*zx, g, d, 0, own).start()
        else:
            arrived(*zx, g, d, r - 1)
            zxr[d, r - 1, g] += own[...]
            hop(*zx, g, d, r).start()

    def xz_send(g, d, r):
        dist = hops(g, d) - r
        k = piece(d, dist)
        own = t_xz(g, owner(d, dist), xlo)
        xp(g, k).wait_recv()
        if r == 0:
            xpr[k, g] += own[...]
            hop(*xz, g, d, 0, xpr.at[k, g]).start()
        else:
            arrived(*xz, g, d, r - 1)
            xzr[d, r - 1, g] += own[...] + xpr[k, g]
            hop(*xz, g, d, r).start()

    def put(ref, x, value):
        for lh in range(2):
            ref[lh, pl.ds(x, 8, stride=16), :] = value[:, 128 * lh:128 * lh + 128]

    def last(buf, sems_s, sems_r, g):
        for d in range(2):
            arrived(buf, sems_s, sems_r, g, d, hops(g, d) - 1)
        return buf[0, hops(g, 0) - 1, g] + buf[1, hops(g, 1) - 1, g]

    def zx_last(g):
        total = t_zx(g, z)[...] + last(*zx, g)
        for q in range(4):
            put(rt0.at[0], 4 * g + q, total[q, :8])
            put(rt0.at[1], 4 * g + q, total[q, 8:])

    def xz_last(g):
        xp(g, 7).wait_recv()
        total = t_xz(g, z, xlo)[...] + xpr[7, g] + last(*xz, g)
        for q in range(4):
            put(rt1, 4 * g + q, total[q])

    def to_even(m):
        side, q = m // 8, (m + j // 2) % 8
        return side, q, jnp.logical_and(side == xlo, 2 * q == j)

    def even_copy(side, q):
        return remote(
            rt0.at[side, :, rows(16 * q, 16)], xr.at[xlo, :, rows(16 * j, 16)],
            b0_s.at[side, q], b_r.at[xlo, j], 2 * z + side, 2 * q,
        )

    def odd_copy(q):
        return remote(
            rt1.at[:, rows(16 * q, 16)], xr.at[0, :, rows(16 * j, 16)],
            b1_s.at[q], b_r.at[0, j], s, 2 * q + 1,
        )

    def even_sends():
        @pl.loop(0, 16)
        def _(m):
            side, q, local = to_even(m)

            @pl.when(jnp.logical_not(local))
            def _():
                even_copy(side, q).start()

        @pl.when(j % 2 == 0)
        def _():
            xr[xlo, :, rows(16 * j, 16)] = rt0[xlo, :, rows(8 * j, 16)]

    def odd_sends():
        @pl.loop(0, 8)
        def _(m):
            q = (m + j // 2) % 8

            @pl.when(2 * q + 1 != j)
            def _():
                odd_copy(q).start()

        @pl.when(j % 2 == 1)
        def _():
            xr[0, :, rows(16 * j, 16)] = rt1[:, rows(8 * (j - 1), 16)]

    def compute(g):
        for c in loads(g):
            c.wait()
        if g == 0:
            tab_copy.wait()

        @pl.loop(4 * g, 4 * g + 4)
        def _(x):
            total = None
            for sub in range(2):
                w = w_v[sub, x]
                slope = jnp.dot(w, tab[6], preferred_element_type=f32)
                term = j_v[sub, x].astype(f32) * (i_v[sub, x].astype(f32) - w.astype(f32)) * slope
                total = term if total is None else total + term
            T[x] = dot3((tab[0], tab[1]), halves(total), ((1,), (1,)))

    act = {
        "zx": zx_send, "xz": xz_send, "xp": lambda g, d, k: xp(g, k).start(),
        "zf": lambda g, d, r: zx_last(g), "xf": lambda g, d, r: xz_last(g),
    }
    computed = summed = 0
    for name, r, g, d in ORDER:
        while computed <= g:
            compute(computed)
            if computed == 0:
                pl.semaphore_wait(barrier, 45)
            computed += 1
        act[name](g, d, r)
        summed += name == "zf"
        if name == "zf" and summed == 4:
            even_sends()
    odd_sends()

    def xr_part(side, src):
        part = xr.at[side, :, rows(16 * src, 16)]
        return remote(part, part, b_r.at[side, src], b_r.at[side, src], s, (j + 1) % 16)

    @pl.loop(0, 16)
    def _(src):
        @pl.when(jnp.logical_or(src != j, jnp.logical_and(j % 2 == 0, xlo == 1)))
        def _():
            xr_part(0, src).wait_recv()

        @pl.when(jnp.logical_and(j % 2 == 0, jnp.logical_or(src != j, xlo == 0)))
        def _():
            xr_part(1, src).wait_recv()

    @pl.when(j % 2 == 0)
    def _():
        xr[0] += xr[1]

    lines = dot3(halves(jnp.concatenate([xr[0, 0], xr[0, 1]], axis=1)), (tab[2], tab[3]))
    spec = dot3((tab[0], tab[1]), halves(lines))
    damp_copy.wait()
    own = damp_v[rows(16 * s + 8 * (j // 8), 8), N:]
    own = jnp.sum(jnp.where(lax.broadcasted_iota(jnp.int32, own.shape, 0) == j % 8, own, 0.0), axis=0, keepdims=True)
    damp = damp_v[:, :N] + jnp.concatenate([own, own], axis=1)
    spec = spec * ((1.0 / sigma_sq) / (damp * damp))
    back = dot3((tab[2], tab[3]), halves(spec))
    field = dot3(halves(back), (tab[0], tab[1]))
    vs[0] = field[:, :128]
    vs[1] = field[:, 128:]

    def back_copy(to):
        return remote(
            vs.at[:, rows(16 * to, 16)], cr.at[:, rows(16 * j, 16)], c_s.at[to], c_r.at[j], s, to
        )

    @pl.loop(1, 16)
    def _(i):
        back_copy((j + i) % 16).start()

    cr[:, rows(16 * j, 16)] = vs[:, rows(16 * j, 16)]

    def depth_copy(half, to):
        return remote(
            ws.at[half, to], dr.at[half, s], d_s.at[half, to], d_r.at[half, s], to, j
        )

    lane = lax.broadcasted_iota(jnp.int32, (8, 128), 1)
    for half in range(2):
        @pl.loop(0, 8)
        def _(q):
            src = 2 * q + half

            @pl.when(src != j)
            def _():
                part = cr.at[:, rows(16 * src, 16)]
                remote(part, part, c_s.at[src], c_r.at[src], s, src).wait_recv()

        parts = []
        for lh in range(2):
            a = [cr[lh, pl.ds(16 * half + x, 8, stride=32), :] for x in range(16)]
            for b in range(3):
                step = 16 << b
                keep = (lane // step) % 2 == 0
                new = list(a)
                for x in range(16):
                    if not x & (1 << b):
                        y = x | (1 << b)
                        new[x] = jnp.where(keep, a[x], pltpu.roll(a[y], step, 1))
                        new[y] = jnp.where(keep, pltpu.roll(a[x], 128 - step, 1), a[y])
                a = new
            parts.append(a)
        for d in range(16):
            for x3 in range(2):
                ws[half, d, :, 128 * x3:128 * x3 + 128] = parts[d // 8][8 * x3 + d % 8]

        @pl.loop(1, 16)
        def _(i):
            depth_copy(half, (s + i) % 16).start()

        dr[half, s] = ws[half, s]

    @pl.loop(1, 16)
    def _(i):
        src = (s + i) % 16
        for half in range(2):
            part = dr.at[half, src]
            remote(part, part, d_s.at[half, src], d_r.at[half, src], src, j).wait_recv()

    res = dot3(halves(dr[...].reshape(N, N)), (tab[4], tab[5]), ((0,), (0,)))
    out_ref[...] = res.reshape(16, 16, N)

    for g in range(4):
        for d in range(2):
            for r in range(hops(g, d)):
                hop(*zx, g, d, r, zxr.at[d, r, g]).wait_send()
                hop(*xz, g, d, r, xzr.at[d, r, g]).wait_send()
        for k in range(8):
            xp(g, k).wait_send()

    @pl.loop(0, 16)
    def _(m):
        side, q, local = to_even(m)

        @pl.when(jnp.logical_not(local))
        def _():
            even_copy(side, q).wait_send()

    @pl.loop(0, 8)
    def _(q):
        @pl.when(2 * q + 1 != j)
        def _():
            odd_copy(q).wait_send()

    @pl.loop(1, 16)
    def _(i):
        back_copy((j + i) % 16).wait_send()
        for half in range(2):
            depth_copy(half, (s + i) % 16).wait_send()


def body(template_warped, subject_images, jacobians, velocity):
    stack, damp = tables()
    dma = pltpu.SemaphoreType.DMA
    any_spec = pl.BlockSpec(memory_space=pltpu.HBM)
    vmem = pl.BlockSpec(memory_space=pltpu.VMEM)
    flat = pltpu.VMEM((2, N, 128), f32)
    inp = pltpu.VMEM((2, 16, N, N), bf16)
    smoothed = pl.pallas_call(
        kernel,
        out_shape=jax.ShapeDtypeStruct((16, 16, N), f32),
        in_specs=[any_spec] * 5,
        out_specs=vmem,
        scratch_shapes=[
            inp, inp, inp,
            pltpu.VMEM((7, N, N), bf16),
            pltpu.VMEM((N, N + 128), f32),
            pltpu.VMEM((16, N, N), f32),
            pltpu.VMEM((2, 4, 4, 4, 16, N), f32),
            pltpu.VMEM((2, 4, 4, 4, 8, N), f32),
            pltpu.VMEM((8, 4, 4, 8, N), f32),
            pltpu.VMEM((2, 2, 128, 128), f32),
            pltpu.VMEM((2, 128, 128), f32),
            pltpu.VMEM((2, 2, N, 128), f32),
            flat, flat,
            pltpu.VMEM((2, 16, 8, N), f32),
            pltpu.VMEM((2, 16, 8, N), f32),
            dma((4, 3)), dma, dma,
            dma((2, 4, 4)), dma((2, 4, 4)), dma((2, 4, 4)), dma((2, 4, 4)),
            dma((8, 4)), dma((8, 4)),
            dma((2, 8)), dma((8,)), dma((2, 16)),
            dma((16,)), dma((16,)), dma((2, 16)), dma((2, 16)),
        ],
        compiler_params=pltpu.CompilerParams(
            collective_id=0, has_side_effects=True, vmem_limit_bytes=67043328
        ),
        name="force_smooth",
    )(
        template_warped, subject_images, jacobians, jnp.asarray(stack), jnp.asarray(damp),
    )
    return velocity - step_size * (2.0 * velocity - smoothed)


def solution(mesh):
    big = P("subj", "space", None, None)
    out = P("space", "subj", None)
    return jax.shard_map(
        body, mesh=mesh, in_specs=(big, big, big, out), out_specs=out, check_vma=False
    )
```

```python
import jax
import jax.numpy as jnp
import numpy as np
from jax import lax
from jax.experimental import pallas as pl
from jax.experimental.pallas import tpu as pltpu
from jax.sharding import PartitionSpec as P

sigma_sq = 0.05
step_size = 0.25
alpha_reach = 16.0

N = 256
RING = 8
ZG = 4
XG = 2
ZP, XP = 16 // ZG, 16 // XG
f32 = jnp.float32
bf16 = jnp.bfloat16
MESH = pl.DeviceIdType.MESH


ORDER = (
    ("zx", 0, 0, 1), ("zx", 0, 0, 0), ("zx", 0, 1, 1), ("xp", 4, 0, 0), ("zx", 0, 1, 0), ("xp", 0, 0, 0),
    ("zx", 0, 2, 1), ("zx", 0, 2, 0), ("xp", 0, 1, 0), ("zx", 0, 3, 1), ("xp", 1, 0, 0), ("zx", 0, 3, 0),
    ("zx", 1, 0, 0), ("xp", 2, 0, 0), ("xp", 2, 1, 0), ("zx", 1, 0, 1), ("zx", 1, 2, 1), ("xz", 0, 0, 0),
    ("zx", 1, 1, 0), ("zx", 1, 3, 1), ("xp", 1, 1, 0), ("zx", 1, 2, 0), ("xz", 0, 1, 1), ("zx", 1, 3, 0),
    ("zx", 2, 0, 0), ("zx", 1, 1, 1), ("xp", 3, 1, 0), ("zx", 2, 2, 1), ("xp", 4, 1, 0), ("xz", 1, 0, 0),
    ("zx", 2, 0, 1), ("zx", 2, 1, 0), ("xp", 5, 0, 0), ("zx", 2, 3, 1), ("xp", 5, 1, 0), ("xp", 6, 0, 0),
    ("xp", 3, 0, 0), ("zx", 2, 2, 0), ("zx", 2, 3, 0), ("xz", 0, 0, 1), ("xz", 1, 1, 1), ("xz", 0, 1, 0),
    ("zx", 3, 2, 1), ("xp", 6, 1, 0), ("xp", 7, 0, 0), ("zx", 3, 3, 1), ("xp", 7, 1, 0), ("zx", 3, 0, 0),
    ("zx", 2, 1, 1), ("zx", 3, 1, 0), ("xz", 2, 0, 0), ("xz", 2, 1, 1), ("xz", 1, 1, 0), ("xz", 1, 0, 1),
    ("zf", 0, 2, 0), ("zf", 0, 3, 0), ("zf", 0, 1, 0), ("zf", 0, 0, 0), ("xz", 3, 1, 1), ("xz", 3, 0, 0),
    ("xz", 2, 0, 1), ("xz", 2, 1, 0), ("xf", 0, 0, 0), ("xf", 0, 1, 0),
)


def tables():
    half = N // 2
    index = np.arange(N)
    freq = np.where(index <= half, index, index - half)
    angle = (index[:, None] * freq[None, :] % N) * (2.0 * np.pi / N)
    wave = np.where(index[None, :] <= half, np.cos(angle), np.sin(angle))
    weight = np.where((index == 0) | (index == half), 1.0, 2.0) / N
    basis = wave * np.sqrt(weight)[None, :]
    lam = 2.0 - 2.0 * np.cos(2.0 * np.pi * freq / N)

    def packed(s, half, q):
        return (s // 2) * 32 + half * 16 + (s % 2) * 8 + q

    s, jj = np.divmod(np.arange(N), 16)
    filtered = packed(s, jj % 2, jj // 2)
    half, s, q = np.arange(N) // 128, np.arange(N) // 8 % 16, np.arange(N) % 8
    gathered = packed(s, half, q)

    def split(a):
        hi = a.astype(np.float32).astype(jnp.bfloat16)
        lo = (a - hi.astype(np.float64)).astype(np.float32).astype(jnp.bfloat16)
        return hi, lo

    stack = []
    for a in (basis.T, basis, basis.T[gathered]):
        stack.extend(split(a))
    shift = np.roll(np.eye(N), 1, axis=0) - np.roll(np.eye(N), -1, axis=0)
    stack.append(shift.astype(jnp.bfloat16))
    damp = 1.0 + alpha_reach * (lam[:, None] + lam[None, :])
    own = np.broadcast_to(alpha_reach * lam[filtered][:, None], (N, 128))
    return np.stack(stack), np.concatenate([damp, own], axis=1).astype(np.float32)


def halves(a):
    hi = a.astype(bf16)
    return hi, (a - hi.astype(f32)).astype(bf16)


def dot3(a, b, dims=((1,), (0,))):
    def one(x, y):
        return lax.dot_general(x, y, (dims, ((), ())), preferred_element_type=f32)

    return one(a[0], b[0]) + (one(a[1], b[0]) + one(a[0], b[1]))


def kernel(
    w_hbm, i_hbm, j_hbm, tab_hbm, damp_hbm, out_ref,
    w_v, i_v, j_v, tab, damp_v, T, zxr, xzr, xpr, rt0, rt1, xr, vs, cr, ws, dr,
    in_sem, tab_sem, damp_sem, zx_s, zx_r, xz_s, xz_r, xp_s, xp_r,
    b0_s, b1_s, b_r, c_s, c_r, d_s, d_r,
):
    s = lax.axis_index("subj")
    j = lax.axis_index("space")
    z = s // 2
    xlo = s % 2
    partner = s + 1 - 2 * xlo

    def dev(ss, jj):
        return {"subj": ss, "space": jj}

    tab_copy = pltpu.make_async_copy(tab_hbm, tab, tab_sem)
    tab_copy.start()

    def loads(g):
        rows = pl.ds(4 * g, 4)
        return [
            pltpu.make_async_copy(h.at[:, rows], v.at[:, rows], in_sem.at[g, a])
            for a, (h, v) in enumerate(((w_hbm, w_v), (i_hbm, i_v), (j_hbm, j_v)))
        ]

    for g in range(4):
        for c in loads(g):
            c.start()
    damp_copy = pltpu.make_async_copy(damp_hbm, damp_v, damp_sem)
    damp_copy.start()

    barrier = pltpu.get_barrier_semaphore()

    @pl.loop(1, 16)
    def _(i):
        pl.semaphore_signal(barrier, inc=1, device_id=dev((s + i) % 16, j), device_id_type=MESH)
        pl.semaphore_signal(barrier, inc=1, device_id=dev(s, (j + i) % 16), device_id_type=MESH)
        pl.semaphore_signal(barrier, inc=1, device_id=dev(partner, (j + i) % 16), device_id_type=MESH)

    def toward(d):
        return (s + 2) % 16 if d == 0 else (s + 14) % 16

    def remote(src, dst, ss, rs, ds, dj):
        return pltpu.make_async_remote_copy(
            src_ref=src, dst_ref=dst, send_sem=ss, recv_sem=rs,
            device_id=dev(ds, dj), device_id_type=MESH,
        )

    def rows(start, size):
        return pl.ds(pl.multiple_of(start, 8), size)

    def hops(buf, g, d):
        return 4 if d == 2 * g // buf.shape[2] else 3

    def owner(d, dist):
        return (z + dist) % RING if d == 0 else (z + RING - dist) % RING

    def t_zx(g, zo):
        return T.at[pl.ds(ZP * g, ZP), rows(32 * zo, 16), :]

    def t_xz(g, zo, side):
        return T.at[pl.ds(XP * g, XP), rows(32 * zo + 16 + 8 * side, 8), :]

    def piece(d, dist):
        return {4: 0, 3: 1 + d, 2: 3 + d, 1: 5 + d, 0: 7}[dist]

    def piece_owner(k):
        return (z, owner(0, 4), owner(0, 3), owner(1, 3), owner(0, 2), owner(1, 2), owner(0, 1), owner(1, 1))[(k + 1) % 8]

    def xp(g, k):
        return remote(t_xz(g, piece_owner(k), 1 - xlo), xpr.at[k, g], xp_s.at[k, g], xp_r.at[k, g], partner, j)

    def hop(buf, ss, rs, g, d, r, src=None):
        src = buf.at[d, r - 1, g] if src is None else src
        return remote(src, buf.at[d, r, g], ss.at[d, r, g], rs.at[d, r, g], toward(d), j)

    def arrived(buf, ss, rs, g, d, r):
        hop(buf, ss, rs, g, d, r, buf.at[d, r, g]).wait_recv()

    zx = (zxr, zx_s, zx_r)
    xz = (xzr, xz_s, xz_r)

    def zx_send(g, d, r):
        own = t_zx(g, owner(d, hops(zxr, g, d) - r))
        if r == 0:
            hop(*zx, g, d, 0, own).start()
        else:
            arrived(*zx, g, d, r - 1)
            zxr[d, r - 1, g] += own[...]
            hop(*zx, g, d, r).start()

    def xz_send(g, d, r):
        dist = hops(xzr, g, d) - r
        k = piece(d, dist)
        own = t_xz(g, owner(d, dist), xlo)
        xp(g, k).wait_recv()
        if r == 0:
            xpr[k, g] += own[...]
            hop(*xz, g, d, 0, xpr.at[k, g]).start()
        else:
            arrived(*xz, g, d, r - 1)
            xzr[d, r - 1, g] += own[...] + xpr[k, g]
            hop(*xz, g, d, r).start()

    def put(ref, x, value):
        for lh in range(2):
            ref[lh, pl.ds(x, 8, stride=16), :] = value[:, 128 * lh:128 * lh + 128]

    def last(buf, sems_s, sems_r, g):
        for d in range(2):
            arrived(buf, sems_s, sems_r, g, d, hops(buf, g, d) - 1)
        return buf[0, hops(buf, g, 0) - 1, g] + buf[1, hops(buf, g, 1) - 1, g]

    def zx_last(g):
        total = t_zx(g, z)[...] + last(*zx, g)
        for x in range(ZP):
            put(rt0.at[0], ZP * g + x, total[x, :8])
            put(rt0.at[1], ZP * g + x, total[x, 8:])

    def xz_last(g):
        xp(g, 7).wait_recv()
        total = t_xz(g, z, xlo)[...] + xpr[7, g] + last(*xz, g)
        for x in range(XP):
            put(rt1, XP * g + x, total[x])

    def to_even(m):
        side, q = m // 8, (m + j // 2) % 8
        return side, q, jnp.logical_and(side == xlo, 2 * q == j)

    def even_copy(side, q):
        return remote(
            rt0.at[side, :, rows(16 * q, 16)], xr.at[xlo, :, rows(16 * j, 16)],
            b0_s.at[side, q], b_r.at[xlo, j], 2 * z + side, 2 * q,
        )

    def odd_copy(q):
        return remote(
            rt1.at[:, rows(16 * q, 16)], xr.at[0, :, rows(16 * j, 16)],
            b1_s.at[q], b_r.at[0, j], s, 2 * q + 1,
        )

    def even_sends():
        @pl.loop(0, 16)
        def _(m):
            side, q, local = to_even(m)

            @pl.when(jnp.logical_not(local))
            def _():
                even_copy(side, q).start()

        @pl.when(j % 2 == 0)
        def _():
            xr[xlo, :, rows(16 * j, 16)] = rt0[xlo, :, rows(8 * j, 16)]

    def odd_sends():
        @pl.loop(0, 8)
        def _(m):
            q = (m + j // 2) % 8

            @pl.when(2 * q + 1 != j)
            def _():
                odd_copy(q).start()

        @pl.when(j % 2 == 1)
        def _():
            xr[0, :, rows(16 * j, 16)] = rt1[:, rows(8 * (j - 1), 16)]

    def compute(g):
        for c in loads(g):
            c.wait()
        if g == 0:
            tab_copy.wait()

        @pl.loop(4 * g, 4 * g + 4)
        def _(x):
            total = None
            for sub in range(2):
                w = w_v[sub, x]
                slope = jnp.dot(w, tab[6], preferred_element_type=f32)
                term = j_v[sub, x].astype(f32) * (i_v[sub, x].astype(f32) - w.astype(f32)) * slope
                total = term if total is None else total + term
            T[x] = dot3((tab[0], tab[1]), halves(total), ((1,), (1,)))

    act = {
        "zx": zx_send, "xz": xz_send, "xp": lambda g, d, k: xp(g, k).start(),
        "zf": lambda g, d, r: zx_last(g), "xf": lambda g, d, r: xz_last(g),
    }
    computed = summed = 0
    for name, r, g, d in ORDER:
        groups = ZG if name[0] == "z" else XG
        while computed < 4 * (g + 1) // groups:
            compute(computed)
            if computed == 0:
                pl.semaphore_wait(barrier, 45)
            computed += 1
        act[name](g, d, r)
        summed += name == "zf"
        if name == "zf" and summed == ZG:
            even_sends()
    odd_sends()

    def xr_part(side, src):
        part = xr.at[side, :, rows(16 * src, 16)]
        return remote(part, part, b_r.at[side, src], b_r.at[side, src], s, (j + 1) % 16)

    @pl.loop(0, 16)
    def _(src):
        @pl.when(jnp.logical_or(src != j, jnp.logical_and(j % 2 == 0, xlo == 1)))
        def _():
            xr_part(0, src).wait_recv()

        @pl.when(jnp.logical_and(j % 2 == 0, jnp.logical_or(src != j, xlo == 0)))
        def _():
            xr_part(1, src).wait_recv()

    @pl.when(j % 2 == 0)
    def _():
        xr[0] += xr[1]

    lines = dot3(halves(jnp.concatenate([xr[0, 0], xr[0, 1]], axis=1)), (tab[2], tab[3]))
    spec = dot3((tab[0], tab[1]), halves(lines))
    damp_copy.wait()
    own = damp_v[rows(16 * s + 8 * (j // 8), 8), N:]
    own = jnp.sum(jnp.where(lax.broadcasted_iota(jnp.int32, own.shape, 0) == j % 8, own, 0.0), axis=0, keepdims=True)
    damp = damp_v[:, :N] + jnp.concatenate([own, own], axis=1)
    spec = spec * ((1.0 / sigma_sq) / (damp * damp))
    back = dot3((tab[2], tab[3]), halves(spec))
    field = dot3(halves(back), (tab[0], tab[1]))
    vs[0] = field[:, :128]
    vs[1] = field[:, 128:]

    def back_copy(to):
        return remote(
            vs.at[:, rows(16 * to, 16)], cr.at[:, rows(16 * j, 16)], c_s.at[to], c_r.at[j], s, to
        )

    @pl.loop(1, 16)
    def _(i):
        back_copy((j + i) % 16).start()

    cr[:, rows(16 * j, 16)] = vs[:, rows(16 * j, 16)]

    def depth_copy(half, to):
        return remote(
            ws.at[half, to], dr.at[half, s], d_s.at[half, to], d_r.at[half, s], to, j
        )

    lane = lax.broadcasted_iota(jnp.int32, (8, 128), 1)
    for half in range(2):
        @pl.loop(0, 8)
        def _(q):
            src = 2 * q + half

            @pl.when(src != j)
            def _():
                part = cr.at[:, rows(16 * src, 16)]
                remote(part, part, c_s.at[src], c_r.at[src], s, src).wait_recv()

        parts = []
        for lh in range(2):
            a = [cr[lh, pl.ds(16 * half + x, 8, stride=32), :] for x in range(16)]
            for b in range(3):
                step = 16 << b
                keep = (lane // step) % 2 == 0
                new = list(a)
                for x in range(16):
                    if not x & (1 << b):
                        y = x | (1 << b)
                        new[x] = jnp.where(keep, a[x], pltpu.roll(a[y], step, 1))
                        new[y] = jnp.where(keep, pltpu.roll(a[x], 128 - step, 1), a[y])
                a = new
            parts.append(a)
        for d in range(16):
            for x3 in range(2):
                ws[half, d, :, 128 * x3:128 * x3 + 128] = parts[d // 8][8 * x3 + d % 8]

        @pl.loop(1, 16)
        def _(i):
            depth_copy(half, (s + i) % 16).start()

        dr[half, s] = ws[half, s]

    @pl.loop(1, 16)
    def _(i):
        src = (s + i) % 16
        for half in range(2):
            part = dr.at[half, src]
            remote(part, part, d_s.at[half, src], d_r.at[half, src], src, j).wait_recv()

    res = dot3(halves(dr[...].reshape(N, N)), (tab[4], tab[5]), ((0,), (0,)))
    out_ref[...] = res.reshape(16, 16, N)

    for one in (zx, xz):
        buf = one[0]
        for g in range(buf.shape[2]):
            for d in range(2):
                for r in range(hops(buf, g, d)):
                    hop(*one, g, d, r, buf.at[d, r, g]).wait_send()
    for g in range(XG):
        for k in range(8):
            xp(g, k).wait_send()

    @pl.loop(0, 16)
    def _(m):
        side, q, local = to_even(m)

        @pl.when(jnp.logical_not(local))
        def _():
            even_copy(side, q).wait_send()

    @pl.loop(0, 8)
    def _(q):
        @pl.when(2 * q + 1 != j)
        def _():
            odd_copy(q).wait_send()

    @pl.loop(1, 16)
    def _(i):
        back_copy((j + i) % 16).wait_send()
        for half in range(2):
            depth_copy(half, (s + i) % 16).wait_send()


def body(template_warped, subject_images, jacobians, velocity):
    stack, damp = tables()
    dma = pltpu.SemaphoreType.DMA
    any_spec = pl.BlockSpec(memory_space=pltpu.HBM)
    vmem = pl.BlockSpec(memory_space=pltpu.VMEM)
    flat = pltpu.VMEM((2, N, 128), f32)
    inp = pltpu.VMEM((2, 16, N, N), bf16)
    smoothed = pl.pallas_call(
        kernel,
        out_shape=jax.ShapeDtypeStruct((16, 16, N), f32),
        in_specs=[any_spec] * 5,
        out_specs=vmem,
        scratch_shapes=[
            inp, inp, inp,
            pltpu.VMEM((7, N, N), bf16),
            pltpu.VMEM((N, N + 128), f32),
            pltpu.VMEM((16, N, N), f32),
            pltpu.VMEM((2, 4, ZG, ZP, 16, N), f32),
            pltpu.VMEM((2, 4, XG, XP, 8, N), f32),
            pltpu.VMEM((8, XG, XP, 8, N), f32),
            pltpu.VMEM((2, 2, 128, 128), f32),
            pltpu.VMEM((2, 128, 128), f32),
            pltpu.VMEM((2, 2, N, 128), f32),
            flat, flat,
            pltpu.VMEM((2, 16, 8, N), f32),
            pltpu.VMEM((2, 16, 8, N), f32),
            dma((4, 3)), dma, dma,
            dma((2, 4, ZG)), dma((2, 4, ZG)), dma((2, 4, XG)), dma((2, 4, XG)),
            dma((8, XG)), dma((8, XG)),
            dma((2, 8)), dma((8,)), dma((2, 16)),
            dma((16,)), dma((16,)), dma((2, 16)), dma((2, 16)),
        ],
        compiler_params=pltpu.CompilerParams(
            collective_id=0, has_side_effects=True, vmem_limit_bytes=(65536 - 10752) << 10
        ),
        name="force_smooth",
    )(
        template_warped, subject_images, jacobians, jnp.asarray(stack), jnp.asarray(damp),
    )
    return velocity - step_size * (2.0 * velocity - smoothed)


def solution(mesh):
    big = P("subj", "space", None, None)
    out = P("space", "subj", None)
    return jax.shard_map(
        body, mesh=mesh, in_specs=(big, big, big, out), out_specs=out, check_vma=False
    )
```

```python
import jax
import jax.numpy as jnp
import numpy as np
from jax import lax
from jax.experimental import pallas as pl
from jax.experimental.pallas import tpu as pltpu
from jax.sharding import PartitionSpec as P

sigma_sq = 0.05
step_size = 0.25
alpha_reach = 16.0

N = 256
RING = 8
ZG = 4
XG = 2
ZP, XP = 16 // ZG, 16 // XG
f32 = jnp.float32
bf16 = jnp.bfloat16
MESH = pl.DeviceIdType.MESH


ORDER = (
    ("zx", 0, 0, 1), ("zx", 0, 0, 0), ("zx", 0, 1, 1), ("xp", 4, 0, 0), ("zx", 0, 1, 0), ("xp", 0, 0, 0),
    ("zx", 0, 2, 1), ("zx", 0, 2, 0), ("xp", 0, 1, 0), ("zx", 0, 3, 1), ("xp", 1, 0, 0), ("zx", 0, 3, 0),
    ("zx", 1, 0, 0), ("xp", 2, 0, 0), ("xp", 2, 1, 0), ("zx", 1, 0, 1), ("zx", 1, 2, 1), ("xz", 0, 0, 0),
    ("zx", 1, 1, 0), ("zx", 1, 3, 1), ("xp", 1, 1, 0), ("zx", 1, 2, 0), ("xz", 0, 1, 1), ("zx", 1, 3, 0),
    ("zx", 2, 0, 0), ("zx", 1, 1, 1), ("xp", 3, 1, 0), ("zx", 2, 2, 1), ("xp", 4, 1, 0), ("xz", 1, 0, 0),
    ("zx", 2, 0, 1), ("zx", 2, 1, 0), ("xp", 5, 0, 0), ("zx", 2, 3, 1), ("xp", 5, 1, 0), ("xp", 6, 0, 0),
    ("xp", 3, 0, 0), ("zx", 2, 2, 0), ("zx", 2, 3, 0), ("xz", 0, 0, 1), ("xz", 1, 1, 1), ("xz", 0, 1, 0),
    ("zx", 3, 2, 1), ("xp", 6, 1, 0), ("xp", 7, 0, 0), ("zx", 3, 3, 1), ("xp", 7, 1, 0), ("zx", 3, 0, 0),
    ("zx", 2, 1, 1), ("zx", 3, 1, 0), ("xz", 2, 0, 0), ("xz", 2, 1, 1), ("xz", 1, 1, 0), ("xz", 1, 0, 1),
    ("zf", 0, 2, 0), ("zf", 0, 3, 0), ("zf", 0, 1, 0), ("zf", 0, 0, 0), ("xz", 3, 1, 1), ("xz", 3, 0, 0),
    ("xz", 2, 0, 1), ("xz", 2, 1, 0), ("xf", 0, 0, 0), ("xf", 0, 1, 0),
)


def tables():
    half = N // 2
    index = np.arange(N)
    freq = np.where(index <= half, index, index - half)
    angle = (index[:, None] * freq[None, :] % N) * (2.0 * np.pi / N)
    wave = np.where(index[None, :] <= half, np.cos(angle), np.sin(angle))
    weight = np.where((index == 0) | (index == half), 1.0, 2.0) / N
    basis = wave * np.sqrt(weight)[None, :]
    lam = 2.0 - 2.0 * np.cos(2.0 * np.pi * freq / N)

    def packed(s, half, q):
        return (s // 2) * 32 + half * 16 + (s % 2) * 8 + q

    s, jj = np.divmod(np.arange(N), 16)
    filtered = packed(s, jj % 2, jj // 2)
    half, s, q = np.arange(N) // 128, np.arange(N) // 8 % 16, np.arange(N) % 8
    gathered = packed(s, half, q)

    def split(a):
        hi = a.astype(np.float32).astype(jnp.bfloat16)
        lo = (a - hi.astype(np.float64)).astype(np.float32).astype(jnp.bfloat16)
        return hi, lo

    stack = []
    for a in (basis.T, basis, basis.T[gathered]):
        stack.extend(split(a))
    shift = np.roll(np.eye(N), 1, axis=0) - np.roll(np.eye(N), -1, axis=0)
    stack.append(shift.astype(jnp.bfloat16))
    damp = 1.0 + alpha_reach * (lam[:, None] + lam[None, :])
    own = np.broadcast_to(alpha_reach * lam[filtered][:, None], (N, 128))
    return np.stack(stack), np.concatenate([damp, own], axis=1).astype(np.float32)


def halves(a):
    hi = a.astype(bf16)
    return hi, (a - hi.astype(f32)).astype(bf16)


def dot3(a, b, dims=((1,), (0,))):
    def one(x, y):
        return lax.dot_general(x, y, (dims, ((), ())), preferred_element_type=f32)

    return one(a[0], b[0]) + (one(a[1], b[0]) + one(a[0], b[1]))


def kernel(
    w_hbm, i_hbm, j_hbm, tab_hbm, damp_hbm, out_ref,
    w_v, i_v, j_v, tab, damp_v, T, zxr, xzr, xpr, rt0, rt1, xr, vs, cr, ws, dr,
    in_sem, tab_sem, damp_sem, zx_s, zx_r, xz_s, xz_r, xp_s, xp_r,
    b0_s, b1_s, b_r, c_s, c_r, d_s, d_r,
):
    s = lax.axis_index("subj")
    j = lax.axis_index("space")
    z = s // 2
    xlo = s % 2
    partner = s + 1 - 2 * xlo

    def dev(ss, jj):
        return {"subj": ss, "space": jj}

    tab_copy = pltpu.make_async_copy(tab_hbm, tab, tab_sem)
    tab_copy.start()

    def loads(g):
        rows = pl.ds(4 * g, 4)
        return [
            pltpu.make_async_copy(h.at[:, rows], v.at[:, rows], in_sem.at[g, a])
            for a, (h, v) in enumerate(((w_hbm, w_v), (i_hbm, i_v), (j_hbm, j_v)))
        ]

    for g in range(4):
        for c in loads(g):
            c.start()
    damp_copy = pltpu.make_async_copy(damp_hbm, damp_v, damp_sem)
    damp_copy.start()

    barrier = pltpu.get_barrier_semaphore()

    @pl.loop(1, 16)
    def _(i):
        pl.semaphore_signal(barrier, inc=1, device_id=dev((s + i) % 16, j), device_id_type=MESH)
        pl.semaphore_signal(barrier, inc=1, device_id=dev(s, (j + i) % 16), device_id_type=MESH)
        pl.semaphore_signal(barrier, inc=1, device_id=dev(partner, (j + i) % 16), device_id_type=MESH)

    def toward(d):
        return (s + 2) % 16 if d == 0 else (s + 14) % 16

    def remote(src, dst, ss, rs, ds, dj):
        return pltpu.make_async_remote_copy(
            src_ref=src, dst_ref=dst, send_sem=ss, recv_sem=rs,
            device_id=dev(ds, dj), device_id_type=MESH,
        )

    def rows(start, size):
        return pl.ds(pl.multiple_of(start, 8), size)

    def hops(buf, g, d):
        return 4 if d == 2 * g // buf.shape[2] else 3

    def owner(d, dist):
        return (z + dist) % RING if d == 0 else (z + RING - dist) % RING

    def t_zx(g, zo):
        return T.at[pl.ds(ZP * g, ZP), rows(32 * zo, 16), :]

    def t_xz(g, zo, side):
        return T.at[pl.ds(XP * g, XP), rows(32 * zo + 16 + 8 * side, 8), :]

    def piece(d, dist):
        return {4: 0, 3: 1 + d, 2: 3 + d, 1: 5 + d, 0: 7}[dist]

    def piece_owner(k):
        return (z, owner(0, 4), owner(0, 3), owner(1, 3), owner(0, 2), owner(1, 2), owner(0, 1), owner(1, 1))[(k + 1) % 8]

    def xp(g, k):
        return remote(t_xz(g, piece_owner(k), 1 - xlo), xpr.at[k, g], xp_s.at[k, g], xp_r.at[k, g], partner, j)

    def hop(buf, ss, rs, g, d, r, src=None):
        src = buf.at[d, r - 1, g] if src is None else src
        return remote(src, buf.at[d, r, g], ss.at[d, r, g], rs.at[d, r, g], toward(d), j)

    def arrived(buf, ss, rs, g, d, r):
        hop(buf, ss, rs, g, d, r, buf.at[d, r, g]).wait_recv()

    zx = (zxr, zx_s, zx_r)
    xz = (xzr, xz_s, xz_r)

    def zx_send(g, d, r):
        own = t_zx(g, owner(d, hops(zxr, g, d) - r))
        if r == 0:
            hop(*zx, g, d, 0, own).start()
        else:
            arrived(*zx, g, d, r - 1)
            zxr[d, r - 1, g] += own[...]
            hop(*zx, g, d, r).start()

    def xz_send(g, d, r):
        dist = hops(xzr, g, d) - r
        k = piece(d, dist)
        own = t_xz(g, owner(d, dist), xlo)
        xp(g, k).wait_recv()
        if r == 0:
            xpr[k, g] += own[...]
            hop(*xz, g, d, 0, xpr.at[k, g]).start()
        else:
            arrived(*xz, g, d, r - 1)
            xzr[d, r - 1, g] += own[...] + xpr[k, g]
            hop(*xz, g, d, r).start()

    def put(ref, x, value):
        for lh in range(2):
            ref[lh, pl.ds(x, 8, stride=16), :] = value[:, 128 * lh:128 * lh + 128]

    def last(buf, sems_s, sems_r, g):
        for d in range(2):
            arrived(buf, sems_s, sems_r, g, d, hops(buf, g, d) - 1)
        return buf[0, hops(buf, g, 0) - 1, g] + buf[1, hops(buf, g, 1) - 1, g]

    def zx_last(g):
        total = t_zx(g, z)[...] + last(*zx, g)
        for x in range(ZP):
            put(rt0.at[0], ZP * g + x, total[x, :8])
            put(rt0.at[1], ZP * g + x, total[x, 8:])

    def xz_last(g):
        xp(g, 7).wait_recv()
        total = t_xz(g, z, xlo)[...] + xpr[7, g] + last(*xz, g)
        for x in range(XP):
            put(rt1, XP * g + x, total[x])

    def to_even(m):
        side, q = m // 8, (m + j // 2) % 8
        return side, q, jnp.logical_and(side == xlo, 2 * q == j)

    def even_copy(side, q):
        return remote(
            rt0.at[side, :, rows(16 * q, 16)], xr.at[xlo, :, rows(16 * j, 16)],
            b0_s.at[side, q], b_r.at[xlo, j], 2 * z + side, 2 * q,
        )

    def odd_copy(q):
        return remote(
            rt1.at[:, rows(16 * q, 16)], xr.at[0, :, rows(16 * j, 16)],
            b1_s.at[q], b_r.at[0, j], s, 2 * q + 1,
        )

    def even_sends():
        @pl.loop(0, 16)
        def _(m):
            side, q, local = to_even(m)

            @pl.when(jnp.logical_not(local))
            def _():
                even_copy(side, q).start()

        @pl.when(j % 2 == 0)
        def _():
            xr[xlo, :, rows(16 * j, 16)] = rt0[xlo, :, rows(8 * j, 16)]

    def odd_sends():
        @pl.loop(0, 8)
        def _(m):
            q = (m + j // 2) % 8

            @pl.when(2 * q + 1 != j)
            def _():
                odd_copy(q).start()

        @pl.when(j % 2 == 1)
        def _():
            xr[0, :, rows(16 * j, 16)] = rt1[:, rows(8 * (j - 1), 16)]

    def compute(g):
        for c in loads(g):
            c.wait()
        if g == 0:
            tab_copy.wait()

        @pl.loop(4 * g, 4 * g + 4)
        def _(x):
            total = None
            for sub in range(2):
                w = w_v[sub, x]
                slope = jnp.dot(w, tab[6], preferred_element_type=f32)
                term = j_v[sub, x].astype(f32) * (i_v[sub, x].astype(f32) - w.astype(f32)) * slope
                total = term if total is None else total + term
            T[x] = dot3((tab[0], tab[1]), halves(total), ((1,), (1,)))

    act = {
        "zx": zx_send, "xz": xz_send, "xp": lambda g, d, k: xp(g, k).start(),
        "zf": lambda g, d, r: zx_last(g), "xf": lambda g, d, r: xz_last(g),
    }
    computed = summed = 0
    for name, r, g, d in ORDER:
        groups = ZG if name[0] == "z" else XG
        while computed < 4 * (g + 1) // groups:
            compute(computed)
            if computed == 0:
                pl.semaphore_wait(barrier, 45)
            computed += 1
        act[name](g, d, r)
        summed += name == "zf"
        if name == "zf" and summed == ZG:
            even_sends()
    odd_sends()

    def xr_part(side, src):
        part = xr.at[side, :, rows(16 * src, 16)]
        return remote(part, part, b_r.at[side, src], b_r.at[side, src], s, (j + 1) % 16)

    @pl.loop(0, 16)
    def _(src):
        @pl.when(jnp.logical_or(src != j, jnp.logical_and(j % 2 == 0, xlo == 1)))
        def _():
            xr_part(0, src).wait_recv()

        @pl.when(jnp.logical_and(j % 2 == 0, jnp.logical_or(src != j, xlo == 0)))
        def _():
            xr_part(1, src).wait_recv()

    @pl.when(j % 2 == 0)
    def _():
        xr[0] += xr[1]

    lines = dot3(halves(jnp.concatenate([xr[0, 0], xr[0, 1]], axis=1)), (tab[2], tab[3]))
    spec = dot3((tab[0], tab[1]), halves(lines))
    damp_copy.wait()
    own = damp_v[rows(16 * s + 8 * (j // 8), 8), N:]
    own = jnp.sum(jnp.where(lax.broadcasted_iota(jnp.int32, own.shape, 0) == j % 8, own, 0.0), axis=0, keepdims=True)
    damp = damp_v[:, :N] + jnp.concatenate([own, own], axis=1)
    spec = spec * ((1.0 / sigma_sq) / (damp * damp))
    back = dot3((tab[2], tab[3]), halves(spec))
    field = dot3(halves(back), (tab[0], tab[1]))
    vs[0] = field[:, :128]
    vs[1] = field[:, 128:]

    def back_copy(to):
        return remote(
            vs.at[:, rows(16 * to, 16)], cr.at[:, rows(16 * j, 16)], c_s.at[to], c_r.at[j], s, to
        )

    @pl.loop(1, 16)
    def _(i):
        back_copy((j + i) % 16).start()

    cr[:, rows(16 * j, 16)] = vs[:, rows(16 * j, 16)]

    def depth_copy(half, to):
        return remote(
            ws.at[half, to], dr.at[half, s], d_s.at[half, to], d_r.at[half, s], to, j
        )

    lane = lax.broadcasted_iota(jnp.int32, (8, 128), 1)
    for half in range(2):
        @pl.loop(0, 8)
        def _(q):
            src = 2 * q + half

            @pl.when(src != j)
            def _():
                part = cr.at[:, rows(16 * src, 16)]
                remote(part, part, c_s.at[src], c_r.at[src], s, src).wait_recv()

        parts = []
        for lh in range(2):
            a = [cr[lh, pl.ds(16 * half + x, 8, stride=32), :] for x in range(16)]
            for b in range(3):
                step = 16 << b
                keep = (lane // step) % 2 == 0
                new = list(a)
                for x in range(16):
                    if not x & (1 << b):
                        y = x | (1 << b)
                        new[x] = jnp.where(keep, a[x], pltpu.roll(a[y], step, 1))
                        new[y] = jnp.where(keep, pltpu.roll(a[x], 128 - step, 1), a[y])
                a = new
            parts.append(a)
        for d in range(16):
            for x3 in range(2):
                ws[half, d, :, 128 * x3:128 * x3 + 128] = parts[d // 8][8 * x3 + d % 8]

        @pl.loop(1, 16)
        def _(i):
            depth_copy(half, (s + i) % 16).start()

        dr[half, s] = ws[half, s]

    res = None
    for half in range(2):
        @pl.loop(1, 16)
        def _(i):
            src = (s + i) % 16
            part = dr.at[half, src]
            remote(part, part, d_s.at[half, src], d_r.at[half, src], src, j).wait_recv()

        k = slice(128 * half, 128 * half + 128)
        term = dot3(halves(dr[half].reshape(128, N)), (tab[4, k], tab[5, k]), ((0,), (0,)))
        res = term if res is None else res + term
    out_ref[...] = res.reshape(16, 16, N)

    for one in (zx, xz):
        buf = one[0]
        for g in range(buf.shape[2]):
            for d in range(2):
                for r in range(hops(buf, g, d)):
                    hop(*one, g, d, r, buf.at[d, r, g]).wait_send()
    for g in range(XG):
        for k in range(8):
            xp(g, k).wait_send()

    @pl.loop(0, 16)
    def _(m):
        side, q, local = to_even(m)

        @pl.when(jnp.logical_not(local))
        def _():
            even_copy(side, q).wait_send()

    @pl.loop(0, 8)
    def _(q):
        @pl.when(2 * q + 1 != j)
        def _():
            odd_copy(q).wait_send()

    @pl.loop(1, 16)
    def _(i):
        back_copy((j + i) % 16).wait_send()
        for half in range(2):
            depth_copy(half, (s + i) % 16).wait_send()


def body(template_warped, subject_images, jacobians, velocity):
    stack, damp = tables()
    dma = pltpu.SemaphoreType.DMA
    any_spec = pl.BlockSpec(memory_space=pltpu.HBM)
    vmem = pl.BlockSpec(memory_space=pltpu.VMEM)
    flat = pltpu.VMEM((2, N, 128), f32)
    inp = pltpu.VMEM((2, 16, N, N), bf16)
    smoothed = pl.pallas_call(
        kernel,
        out_shape=jax.ShapeDtypeStruct((16, 16, N), f32),
        in_specs=[any_spec] * 5,
        out_specs=vmem,
        scratch_shapes=[
            inp, inp, inp,
            pltpu.VMEM((7, N, N), bf16),
            pltpu.VMEM((N, N + 128), f32),
            pltpu.VMEM((16, N, N), f32),
            pltpu.VMEM((2, 4, ZG, ZP, 16, N), f32),
            pltpu.VMEM((2, 4, XG, XP, 8, N), f32),
            pltpu.VMEM((8, XG, XP, 8, N), f32),
            pltpu.VMEM((2, 2, 128, 128), f32),
            pltpu.VMEM((2, 128, 128), f32),
            pltpu.VMEM((2, 2, N, 128), f32),
            flat, flat,
            pltpu.VMEM((2, 16, 8, N), f32),
            pltpu.VMEM((2, 16, 8, N), f32),
            dma((4, 3)), dma, dma,
            dma((2, 4, ZG)), dma((2, 4, ZG)), dma((2, 4, XG)), dma((2, 4, XG)),
            dma((8, XG)), dma((8, XG)),
            dma((2, 8)), dma((8,)), dma((2, 16)),
            dma((16,)), dma((16,)), dma((2, 16)), dma((2, 16)),
        ],
        compiler_params=pltpu.CompilerParams(
            collective_id=0, has_side_effects=True, vmem_limit_bytes=(65536 - 10752) << 10
        ),
        name="force_smooth",
    )(
        template_warped, subject_images, jacobians, jnp.asarray(stack), jnp.asarray(damp),
    )
    return velocity - step_size * (2.0 * velocity - smoothed)


def solution(mesh):
    big = P("subj", "space", None, None)
    out = P("space", "subj", None)
    return jax.shard_map(
        body, mesh=mesh, in_specs=(big, big, big, out), out_specs=out, check_vma=False
    )
```
